1024 devices in a mesh: gx: 8 (over y), gy: 4 (over x), gz: 32 (over z, core).
Axes of the slice: x: 4, y: 8, z: 16, core: 2. Of those that a mesh axis runs over, the one named last changes fastest.
Arguments:
- rhs: float32 [8, 4, 32, 2, 64, 256], P('gx', 'gy', 'gz'), may hold values from -6 to 6
- viscosity: float32 [8, 4, 32, 64], P('gx', 'gy', 'gz'), may hold values from 0.3 to 3
- counts: int32 [8, 4, 32], P('gx', 'gy', 'gz'), may hold values from 8 to 64, as said below
- neighbours: int32 [8, 4, 32, 16], P('gx', 'gy', 'gz'), may hold values from -1 to 31, as said below
- face_index: int32 [8, 4, 32, 16, 512], P('gx', 'gy', 'gz'), may hold values from 0 to 16383, as said below
- k_matrix: float32 [256, 256], replicated, may hold values from -0.04 to 1.04, as said below
- p_matrix: float32 [256, 256], replicated, may hold values from -0.04 to 1.04, as said below
Outputs:
- solution: float32 [8, 4, 32, 2, 64, 256], P('gx', 'gy', 'gz')
The draws below stay inside these ranges and needn't reach their ends.
Inputs may be any that keep to these rules, and one draw needn't show every extreme that they name: `counts`: in every gz group some partition has exactly 64 live elements. `neighbours`: each list names distinct partitions of the same gz group in increasing order, followed by -1 entries; the relation is symmetric and no partition names itself. `face_index`: every index lies within the live elements of its partition, that is below 256 times counts. `k_matrix`: the identity plus independent entries. `p_matrix`: the identity plus independent entries.
All inputs are finite; a program needn't handle non-finite values.
Results may differ from the reference program's by a relative error of at most 0.0003.
Values sent between devices are 32-bit elements; how exact they have to be, the bound alone decides.
A program may use at most 32 MiB of HBM per device.

```python
import math
import jax
import jax.numpy as jnp
from jax import lax

E_DEV = 64
EDOF = 256
PROBES = 2
NBR = 16
FACE = 512
N_GX = 8
N_GY = 4
N_GZ = 32


def draw_block(key, salt):
    noise = jax.random.uniform(jax.random.fold_in(key, salt), (EDOF, EDOF), jnp.float32, -0.0325, 0.0325)
    return jnp.eye(EDOF, dtype=jnp.float32) + noise


def draw_k_matrix(key, part):
    return draw_block(key, 101)


def draw_p_matrix(key, part):
    return draw_block(key, 202)


def live_counts(key):
    inner_key = jax.random.fold_in(key, 303)
    shifts = jax.random.randint(jax.random.fold_in(inner_key, 1), (N_GX, N_GY, N_GZ), 0, 4)
    chosen = jax.random.randint(jax.random.fold_in(inner_key, 2), (N_GX, N_GY, 1), 0, N_GZ)
    places = jnp.arange(N_GZ, dtype=jnp.int32)[None, None, :]
    shifts = jnp.where(places == chosen, 0, shifts)
    return (E_DEV // jnp.left_shift(jnp.ones_like(shifts), shifts)).astype(jnp.int32)


def draw_counts(key, part):
    return live_counts(key)


def draw_face_index(key, part):
    bounds = (live_counts(key) * EDOF)[:, :, :, None, None]
    return jax.random.randint(jax.random.fold_in(key, 404), (N_GX, N_GY, N_GZ, NBR, FACE), 0, bounds).astype(jnp.int32)


def group_links(key):
    members = N_GZ
    adjacency = jnp.zeros((members, members), jnp.int32)
    cycles = max(1, min(NBR // 2, members // 4))
    for turn in range(cycles):
        order = jax.random.permutation(jax.random.fold_in(key, turn), members)
        after = jnp.roll(order, -1)
        adjacency = adjacency.at[order, after].set(1)
        adjacency = adjacency.at[after, order].set(1)
    columns = jnp.arange(members, dtype=jnp.int32)
    scores = (1 - adjacency) * members + columns[None, :]
    ranked = jnp.argsort(scores, axis=1, stable=True).astype(jnp.int32)
    keep = min(members, NBR)
    ranked = jnp.pad(ranked[:, :keep], ((0, 0), (0, NBR - keep)), constant_values=-1)
    degree = jnp.sum(adjacency, axis=1)
    slots = jnp.arange(NBR, dtype=jnp.int32)
    return jnp.where(slots[None, :] < degree[:, None], ranked, -1).astype(jnp.int32)


def draw_neighbours(key, part):
    keys = jax.random.split(jax.random.fold_in(key, 505), N_GX * N_GY)
    return jax.vmap(group_links)(keys).reshape(N_GX, N_GY, N_GZ, NBR)


def shard_levels(own_key, extent, cuts, least, top_value):
    def one(position, shards_of):
        heights = jax.random.uniform(jax.random.fold_in(jax.random.fold_in(own_key, 6), position), (shards_of,), jnp.float32, least / len(cuts), top_value / len(cuts))
        return jnp.repeat(jnp.exp(heights), extent[position] // shards_of).reshape((-1,) + (1,) * (len(extent) - position - 1))

    gain = one(*cuts[0])
    for cut in cuts[1:]:
        gain = gain * one(*cut)
    return gain


def bell_draw(rng, extent, spread, limit, pieces=(), kind=jnp.bfloat16):
    entries = spread * jax.random.normal(rng, extent, jnp.float32)
    if pieces:
        entries = entries * shard_levels(rng, extent, pieces, -0.22, 0.18)
    return jnp.clip(entries, -limit, limit).astype(kind)


def setup_inputs(seed: int = 0) -> dict:
    arg_keys = jax.random.split(jax.random.key(seed), 8)
    return {
        "rhs": bell_draw(arg_keys[0], (N_GX, N_GY, N_GZ, PROBES, E_DEV, EDOF), 1.0, 6.0, ((0, 8), (1, 4), (2, 32)), jnp.float32),
        "viscosity": jnp.clip(jnp.exp(math.log(3.0) - 2.3025851 * jax.random.uniform(arg_keys[1], (N_GX, N_GY, N_GZ, E_DEV), jnp.float32) ** shard_levels(arg_keys[1], (N_GX, N_GY, N_GZ, E_DEV), ((0, 8), (1, 4), (2, 32)), -0.2, 0.2)), 0.3, 3.0),
        "counts": draw_counts(jax.random.fold_in(arg_keys[7], 71), 0),
        "neighbours": draw_neighbours(jax.random.fold_in(arg_keys[7], 71), 0),
        "face_index": draw_face_index(jax.random.fold_in(arg_keys[7], 71), 0),
        "k_matrix": draw_k_matrix(jax.random.fold_in(arg_keys[7], 71), 0),
        "p_matrix": draw_p_matrix(jax.random.fold_in(arg_keys[7], 71), 0),
    }


coupling = 0.5
largest_rank = lax.Precision.HIGHEST


def per_element(vector, matrix):
    shaped = vector.shape
    product = jnp.dot(vector.reshape(-1, shaped[-1]), matrix, precision=largest_rank, preferred_element_type=jnp.float32)
    return product.reshape(shaped)


def face_term(vector, links, blocks):
    members, probes, elements, dofs = vector.shape
    flat_vec = vector.reshape(members, probes, elements * dofs)

    def take_faces(row_vals, index):
        return row_vals[:, index.reshape(-1)].reshape(probes, index.shape[0], index.shape[1])

    departing_rows = jax.vmap(take_faces)(flat_vec, blocks)
    sources = jnp.arange(members, dtype=jnp.int32)
    connected_parts = (links[:, :, None] == sources[None, None, :]).astype(jnp.float32)
    received_rows = jnp.einsum("bon,nlb,nzla->bzoa", connected_parts, connected_parts, departing_rows, precision=largest_rank)

    def place(value_list, index):
        empty = jnp.zeros((probes, elements * dofs), jnp.float32)
        return empty.at[:, index.reshape(-1)].add(value_list.reshape(probes, -1))

    placed = jax.vmap(place)(received_rows, blocks)
    return placed.reshape(vector.shape)


def group_pass(group, k_matrix, p_matrix):
    vector, visc, live_count, links, blocks = group
    elements = vector.shape[2]
    live_mask = (jnp.arange(elements, dtype=jnp.int32)[None, :] < live_count[:, None]).astype(jnp.float32)[:, None, :, None]
    visc_col = visc[:, None, :, None]
    source = vector * live_mask

    def smooth(field_in):
        return per_element(field_in, p_matrix) / visc_col * live_mask

    def apply_op(field_in):
        return (per_element(field_in, k_matrix) * visc_col - coupling * face_term(field_in, links, blocks)) * live_mask

    def inner_prod(left_vec, right_vec):
        return jnp.sum(left_vec * right_vec, axis=(0, 2, 3))

    first_pre = smooth(source)
    first_img = apply_op(first_pre)
    second_pre = smooth(first_img)
    second_img = apply_op(second_pre)
    matrix_entries = jnp.stack([inner_prod(first_img, first_img), inner_prod(first_img, second_img), inner_prod(second_img, second_img), inner_prod(first_img, source), inner_prod(second_img, source)])
    return first_pre, second_pre, matrix_entries


def reference(rhs, viscosity, counts, neighbours, face_index, k_matrix, p_matrix):
    groups = N_GX * N_GY
    stacked = (rhs.reshape(groups, N_GZ, PROBES, E_DEV, EDOF), viscosity.reshape(groups, N_GZ, E_DEV), counts.reshape(groups, N_GZ), neighbours.reshape(groups, N_GZ, NBR), face_index.reshape(groups, N_GZ, NBR, FACE))
    first_pre, second_pre, matrix_entries = lax.map(lambda group: group_pass(group, k_matrix, p_matrix), stacked)
    totals = jnp.sum(matrix_entries, axis=0)
    self_one, cross_mid, self_two, load_one, load_two = totals[0], totals[1], totals[2], totals[3], totals[4]
    determinant = self_one * self_two - cross_mid * cross_mid
    weight_one = (self_two * load_one - cross_mid * load_two) / determinant
    weight_two = (self_one * load_two - cross_mid * load_one) / determinant
    solution = weight_one[:, None, None] * first_pre + weight_two[:, None, None] * second_pre
    return solution.reshape(N_GX, N_GY, N_GZ, PROBES, E_DEV, EDOF)
```

```python
import functools

import jax
import jax.numpy as jnp
from jax import lax
from jax.experimental import pallas as pl
from jax.experimental.pallas import tpu as pltpu
from jax.sharding import PartitionSpec as P

MESH = pl.DeviceIdType.MESH
coupling = 0.5
LANES = 128
f32 = jnp.float32
bf16 = jnp.bfloat16


def halves(x):
    high = x.astype(bf16)
    low = (x - high.astype(f32)).astype(bf16)
    return high, low


def nn_dot(a, b):
    return lax.dot_general(a, b, (((1,), (0,)), ((), ())), preferred_element_type=f32)


def nt_dot(a, b):
    return lax.dot_general(a, b, (((1,), (1,)), ((), ())), preferred_element_type=f32)


def kernel(
    nx, ny, nz, slots, probes, elements, dofs, width,
    rhs_hbm, visc_hbm, counts_hbm, links_hbm, index_hbm, k_hbm, p_hbm,
    out_ref,
    rhs, visc, counts, links, index, k_raw, p_raw,
    k_high, k_low, p_high, p_low, onehot, faces, departing, arriving_a, arriving_b, placed,
    sums_z, sums_xy, load_sems, send_sems, recv_sems,
):
    ix, iy, me = lax.axis_index("gx"), lax.axis_index("gy"), lax.axis_index("gz")
    nxy = nx * ny
    plane = ix * ny + iy
    rows = probes * elements
    pieces = width // LANES

    def z_peer(j):
        half = nz // 2
        offset = half + ((j + 1) // 2) * (1 - 2 * (j % 2))
        return lax.rem(me + offset, nz)

    def xy_peer(j):
        return lax.rem(plane + 1 + j, nxy)

    barrier = pltpu.get_barrier_semaphore()

    def greet_z(j, carry):
        pl.semaphore_signal(barrier, inc=1, device_id=(ix, iy, z_peer(j)), device_id_type=MESH)
        return carry

    def greet_xy(j, carry):
        other = xy_peer(j)
        pl.semaphore_signal(barrier, inc=1, device_id=(other // ny, other % ny, me), device_id_type=MESH)
        return carry

    loads = [
        pltpu.make_async_copy(src, dst, load_sems.at[i])
        for i, (src, dst) in enumerate(
            (
                (index_hbm, index), (rhs_hbm, rhs), (p_hbm, p_raw), (visc_hbm, visc),
                (counts_hbm, counts), (links_hbm, links), (k_hbm, k_raw),
            )
        )
    ]
    for load in loads:
        load.start()
    lax.fori_loop(0, nz - 1, greet_z, 0)
    lax.fori_loop(0, nxy - 1, greet_xy, 0)

    loads[3].wait()
    loads[4].wait()
    loads[5].wait()
    element_id = lax.broadcasted_iota(jnp.int32, (elements, 1), 0)
    live = (element_id < counts[0:1, 0:1]).astype(f32)
    diagonal = lax.broadcasted_iota(jnp.int32, (elements, elements), 0) == lax.broadcasted_iota(
        jnp.int32, (elements, elements), 1
    )
    visc_col = jnp.sum(jnp.where(diagonal, visc[0:1, :], 0.0), axis=1, keepdims=True)
    live_rows = jnp.concatenate([live] * probes, axis=0)
    visc_rows = jnp.concatenate([visc_col] * probes, axis=0)
    inverse_rows = live_rows / visc_rows

    loads[1].wait()
    loads[2].wait()
    p_high[...], p_low[...] = halves(p_raw[...])
    source = jnp.where(live_rows > 0.0, rhs[...], 0.0)

    def per_element(x, m_high, m_low):
        high, low = halves(x)
        both = nn_dot(jnp.concatenate([high, low], axis=0), m_high[...])
        return both[:rows] + both[rows:] + nn_dot(high, m_low[...])

    link_of = [jnp.broadcast_to(links[0:1, l : l + 1], (8, LANES)) for l in range(slots)]

    def gather(x, first):
        stacked = jnp.concatenate(halves(x), axis=0)

        def one_slot(l, carry):
            where_to = index[pl.ds(l, 1), :]
            if first:
                dof = where_to % dofs if dofs & (dofs - 1) else where_to & (dofs - 1)
                ids = lax.broadcasted_iota(jnp.int32, (dofs, width), 0)
                hot = jnp.where(dof == ids, 1.0, 0.0).astype(bf16)
                onehot[l] = hot
            else:
                hot = onehot[l]
            spread = nn_dot(stacked, hot)
            spread = spread[:rows] + spread[rows:]
            chosen = lax.shift_right_logical(where_to, 8) == lax.broadcasted_iota(jnp.int32, (elements, width), 0)
            picked = [
                jnp.sum(jnp.where(chosen, spread[p * elements : (p + 1) * elements], 0.0), axis=0, keepdims=True)
                for p in range(probes)
            ]
            faces[l] = jnp.concatenate(
                [picked[p][:, j * LANES : (j + 1) * LANES] for j in range(pieces) for p in range(probes)], axis=0
            )
            return carry

        lax.fori_loop(0, slots, one_slot, 0)

    def exchange(step, arriving):
        face_blocks = [faces[l] for l in range(slots)]

        def fill(d, carry):
            block = jnp.zeros((8, LANES), f32)
            for l in range(slots):
                block = jnp.where(link_of[l] == d, face_blocks[l], block)
            departing[step, d] = block
            return carry

        lax.fori_loop(0, nz, fill, 0)
        arriving[me] = jnp.zeros((8, LANES), f32)
        if step == 0:
            pl.semaphore_wait(barrier, nz - 1 + nxy - 1)

        def send(j, carry):
            peer = z_peer(j)
            pltpu.make_async_remote_copy(
                src_ref=departing.at[step, peer],
                dst_ref=arriving.at[me],
                send_sem=send_sems.at[step],
                recv_sem=recv_sems.at[step],
                device_id=(ix, iy, peer),
                device_id_type=MESH,
            ).start()
            return carry

        lax.fori_loop(0, nz - 1, send, 0)

    def land(buffer, sem, count):
        pltpu.make_async_copy(buffer.at[pl.ds(0, count)], buffer.at[pl.ds(0, count)], sem).wait()

    def scatter(step, arriving):
        land(arriving, recv_sems.at[step], nz - 1)

        def pick(s, blocks):
            block = arriving[s]
            return tuple(jnp.where(link_of[l] == s, block, blocks[l]) for l in range(slots))

        received = lax.fori_loop(0, nz, pick, tuple(jnp.zeros((8, LANES), f32) for _ in range(slots)))
        for l in range(slots):
            faces[l] = received[l]
        placed[...] = jnp.zeros_like(placed)

        def one_slot(l, carry):
            where_to = index[pl.ds(l, 1), :]
            chosen = lax.shift_right_logical(where_to, 8) == lax.broadcasted_iota(jnp.int32, (elements, width), 0)
            high = faces[l].astype(bf16).astype(f32)
            low = faces[l] - high
            spread = jnp.concatenate(
                [
                    jnp.where(
                        chosen,
                        jnp.concatenate([part[j * probes + p : j * probes + p + 1] for j in range(pieces)], axis=1),
                        0.0,
                    )
                    for part in (high, low)
                    for p in range(probes)
                ],
                axis=0,
            ).astype(bf16)
            placed[...] += nt_dot(spread, onehot[l])
            return carry

        lax.fori_loop(0, slots, one_slot, 0)
        return placed[:rows] + placed[rows:]

    loads[0].wait()
    first_pre = per_element(source, p_high, p_low) * inverse_rows
    gather(first_pre, True)
    exchange(0, arriving_a)
    loads[6].wait()
    k_high[...], k_low[...] = halves(k_raw[...])
    local_part = per_element(first_pre, k_high, k_low) * visc_rows
    first_img = (local_part - coupling * scatter(0, arriving_a)) * live_rows
    second_pre = per_element(first_img, p_high, p_low) * inverse_rows
    gather(second_pre, False)
    exchange(1, arriving_b)
    local_part = per_element(second_pre, k_high, k_low) * visc_rows
    second_img = (local_part - coupling * scatter(1, arriving_b)) * live_rows

    lane = lax.broadcasted_iota(jnp.int32, (1, LANES), 1)
    partial = jnp.zeros((1, LANES), f32)
    pairs = (
        (first_img, first_img), (first_img, second_img), (second_img, second_img),
        (first_img, source), (second_img, source),
    )
    for q, (a, b) in enumerate(pairs):
        product = a * b
        for p in range(probes):
            column = jnp.sum(product[p * elements : (p + 1) * elements], axis=0, keepdims=True)
            value = jnp.sum(column, axis=1, keepdims=True)
            partial = jnp.where(lane == q * probes + p, value, partial)

    def all_sum(buffer, mine, count, stage, device_of, part):
        buffer[mine] = part

        def send(j, carry):
            pltpu.make_async_remote_copy(
                src_ref=buffer.at[mine],
                dst_ref=buffer.at[mine],
                send_sem=send_sems.at[stage],
                recv_sem=recv_sems.at[stage],
                device_id=device_of(j),
                device_id_type=MESH,
            ).start()
            return carry

        lax.fori_loop(0, count - 1, send, 0)
        land(buffer, recv_sems.at[stage], count - 1)
        total = buffer[0]
        for s in range(1, count):
            total = total + buffer[s]
        return total

    def xy_device(j):
        other = xy_peer(j)
        return (other // ny, other % ny, me)

    total = all_sum(sums_z, me, nz, 2, lambda j: (ix, iy, z_peer(j)), partial)
    total = all_sum(sums_xy, plane, nxy, 3, xy_device, total)

    for p in range(probes):
        self_one, cross_mid, self_two, load_one, load_two = (
            jnp.sum(jnp.where(lane == q * probes + p, total, 0.0), axis=1, keepdims=True) for q in range(5)
        )
        determinant = self_one * self_two - cross_mid * cross_mid
        weight_one = (self_two * load_one - cross_mid * load_two) / determinant
        weight_two = (self_one * load_two - cross_mid * load_one) / determinant
        part = slice(p * elements, (p + 1) * elements)
        out_ref[part] = weight_one * first_pre[part] + weight_two * second_pre[part]

    land(departing.at[0], send_sems.at[0], nz - 1)
    land(departing.at[1], send_sems.at[1], nz - 1)
    land(sums_z, send_sems.at[2], nz - 1)
    land(sums_xy, send_sems.at[3], nxy - 1)


def solution(mesh):
    nx, ny, nz = (mesh.shape[name] for name in ("gx", "gy", "gz"))

    def per_device(rhs, viscosity, counts, neighbours, face_index, k_matrix, p_matrix):
        probes, elements, dofs = rhs.shape[3:]
        slots, width = face_index.shape[3:]
        rows = probes * elements
        vmem = pltpu.VMEM
        any_space = pl.BlockSpec(memory_space=pl.ANY)
        out = pl.pallas_call(
            functools.partial(kernel, nx, ny, nz, slots, probes, elements, dofs, width),
            out_shape=jax.ShapeDtypeStruct((rows, dofs), f32),
            in_specs=[any_space] * 7,
            out_specs=pl.BlockSpec(memory_space=vmem),
            scratch_shapes=[
                vmem((rows, dofs), f32),
                vmem((1, elements), f32),
                vmem((1, 1), jnp.int32),
                vmem((1, slots), jnp.int32),
                vmem((slots, width), jnp.int32),
                vmem((dofs, dofs), f32),
                vmem((dofs, dofs), f32),
                vmem((dofs, dofs), bf16),
                vmem((dofs, dofs), bf16),
                vmem((dofs, dofs), bf16),
                vmem((dofs, dofs), bf16),
                vmem((slots, dofs, width), bf16),
                vmem((slots, 8, LANES), f32),
                vmem((2, nz, 8, LANES), f32),
                vmem((nz, 8, LANES), f32),
                vmem((nz, 8, LANES), f32),
                vmem((2 * rows, dofs), f32),
                vmem((nz, 1, LANES), f32),
                vmem((nx * ny, 1, LANES), f32),
                pltpu.SemaphoreType.DMA((7,)),
                pltpu.SemaphoreType.DMA((4,)),
                pltpu.SemaphoreType.DMA((4,)),
            ],
            compiler_params=pltpu.CompilerParams(collective_id=0, has_side_effects=True),
        )(
            rhs.reshape(rows, dofs),
            viscosity.reshape(1, elements),
            counts.reshape(1, 1),
            neighbours.reshape(1, slots),
            face_index.reshape(slots, width),
            k_matrix,
            p_matrix,
        )
        return out.reshape(rhs.shape)

    return jax.shard_map(
        per_device,
        mesh=mesh,
        in_specs=(
            P("gx", "gy", "gz", None, None, None),
            P("gx", "gy", "gz", None),
            P("gx", "gy", "gz"),
            P("gx", "gy", "gz", None),
            P("gx", "gy", "gz", None, None),
            P(),
            P(),
        ),
        out_specs=P("gx", "gy", "gz", None, None, None),
        check_vma=False,
    )
```

```python
import functools

import jax
import jax.numpy as jnp
from jax import lax
from jax.experimental import pallas as pl
from jax.experimental.pallas import tpu as pltpu
from jax.sharding import PartitionSpec as P

MESH = pl.DeviceIdType.MESH
coupling = 0.5
LANES = 128
f32 = jnp.float32
bf16 = jnp.bfloat16


def halves(x):
    high = x.astype(bf16)
    low = (x - high.astype(f32)).astype(bf16)
    return high, low


def nn_dot(a, b):
    return lax.dot_general(a, b, (((1,), (0,)), ((), ())), preferred_element_type=f32)


def nt_dot(a, b):
    return lax.dot_general(a, b, (((1,), (1,)), ((), ())), preferred_element_type=f32)


def kernel(
    nx, ny, nz, slots, probes, elements, dofs, width,
    rhs_hbm, visc_hbm, counts_hbm, links_hbm, index_hbm, k_hbm, p_hbm,
    pre_one_out, pre_two_out, weights_ref,
    rhs, visc, counts, links, index, k_raw, p_raw,
    k_high, k_low, p_high, p_low, peer_index, onehot, onehot_t, faces, departing, arriving, placed,
    pre_one, pre_two, sums_z, sums_xy, load_sems, out_sems, send_sems, recv_sems, sum_sems,
):
    ix, iy, me = lax.axis_index("gx"), lax.axis_index("gy"), lax.axis_index("gz")
    chip, core = me // 2, me % 2
    chips = nz // 2
    half = chips // 2
    nxy = nx * ny
    plane = ix * ny + iy
    rows = probes * elements
    pieces = width // LANES
    span = 4 * width
    shift = dofs.bit_length() - 1

    def z_peer(j):
        offset = nz // 2 + ((j + 1) // 2) * (1 - 2 * (j % 2))
        return lax.rem(me + offset, nz)

    def xy_peer(j):
        return lax.rem(plane + 1 + j, nxy)

    def group_chip(group, side):
        away = group + 1
        offset = away if side == 0 else -away * (1 - away // half)
        return lax.rem(chip + offset + chips, chips)

    barrier = pltpu.get_barrier_semaphore()

    def greet_z(j, carry):
        pl.semaphore_signal(barrier, inc=1, device_id=(ix, iy, z_peer(j)), device_id_type=MESH)
        return carry

    def greet_xy(j, carry):
        other = xy_peer(j)
        pl.semaphore_signal(barrier, inc=1, device_id=(other // ny, other % ny, me), device_id_type=MESH)
        return carry

    loads = [
        pltpu.make_async_copy(src, dst, load_sems.at[i])
        for i, (src, dst) in enumerate(
            (
                (index_hbm, index), (rhs_hbm, rhs), (p_hbm, p_raw), (visc_hbm, visc),
                (counts_hbm, counts), (links_hbm, links), (k_hbm, k_raw),
            )
        )
    ]
    for load in loads:
        load.start()
    lax.fori_loop(0, nz - 1, greet_z, 0)
    lax.fori_loop(0, nxy - 1, greet_xy, 0)

    loads[3].wait()
    loads[4].wait()
    loads[5].wait()
    element_id = lax.broadcasted_iota(jnp.int32, (elements, 1), 0)
    live = (element_id < counts[0:1, 0:1]).astype(f32)
    diagonal = lax.broadcasted_iota(jnp.int32, (elements, elements), 0) == lax.broadcasted_iota(
        jnp.int32, (elements, elements), 1
    )
    visc_col = jnp.sum(jnp.where(diagonal, visc[0:1, :], 0.0), axis=1, keepdims=True)
    live_rows = jnp.concatenate([live] * probes, axis=0)
    visc_rows = jnp.concatenate([visc_col] * probes, axis=0)
    inverse_rows = live_rows / visc_rows

    loads[1].wait()
    loads[2].wait()
    p_high[...], p_low[...] = halves(p_raw[...])
    source = jnp.where(live_rows > 0.0, rhs[...], 0.0)

    def per_element(x, m_high, m_low):
        high, low = halves(x)
        both = nn_dot(jnp.concatenate([high, low], axis=0), m_high[...])
        return both[:rows] + both[rows:] + nn_dot(high, m_low[...])

    link_of = [jnp.broadcast_to(links[0:1, l : l + 1], (8, LANES)) for l in range(slots)]

    def hot_of(row):
        ids = lax.broadcasted_iota(jnp.int32, (dofs, row.shape[1]), 0)
        return jnp.where((row & (dofs - 1)) == ids, 1.0, 0.0).astype(bf16)

    def chosen_of(row):
        return lax.shift_right_arithmetic(row, shift) == lax.broadcasted_iota(jnp.int32, (elements, row.shape[1]), 0)

    def pick_faces(stacked, hot, row):
        spread = nn_dot(stacked, hot)
        spread = spread[:rows] + spread[rows:]
        chosen = chosen_of(row)
        picked = [
            jnp.sum(jnp.where(chosen, spread[p * elements : (p + 1) * elements], 0.0), axis=0, keepdims=True)
            for p in range(probes)
        ]
        return jnp.concatenate(
            [picked[p][:, j * LANES : (j + 1) * LANES] for j in range(pieces) for p in range(probes)], axis=0
        )

    def gather_slots(x):
        stacked = jnp.concatenate(halves(x), axis=0)

        def one_slot(l, carry):
            row = index[pl.ds(l, 1), :]
            faces[l] = pick_faces(stacked, hot_of(row), row)
            return carry

        lax.fori_loop(0, slots, one_slot, 0)

    def fill_departing():
        face_blocks = [faces[l] for l in range(slots)]

        def fill_group(group, carry):
            for side in range(2):
                for other in range(2):
                    peer = group_chip(group, side) * 2 + other
                    block = jnp.zeros((8, LANES), f32)
                    for l in range(slots):
                        block = jnp.where(link_of[l] == peer, face_blocks[l], block)
                    departing[0, group * 4 + side * 2 + other] = block
            return carry

        lax.fori_loop(0, half, fill_group, 0)

    def send_one(step, group, side, other, landing_side):
        pltpu.make_async_remote_copy(
            src_ref=departing.at[step, group * 4 + side * 2 + other],
            dst_ref=arriving.at[step, group * 4 + landing_side * 2 + core],
            send_sem=send_sems.at[step],
            recv_sem=recv_sems.at[step, group],
            device_id=(ix, iy, group_chip(group, side) * 2 + other),
            device_id_type=MESH,
        ).start()

    def send_last(step):
        send_one(step, half - 1, 0, 0, 0)
        send_one(step, half - 1, 0, 1, 0)
        send_one(step, half - 1, 1, 1 - core, 1)

    def send_group(step, group):
        for side in range(2):
            for other in range(2):
                send_one(step, group, side, other, 1 - side)

    def group_row(group):
        return jnp.concatenate([peer_index[pl.ds(group * 4 + r, 1), :] for r in range(4)], axis=1)

    def make_peer_index():
        peer_number = lax.broadcasted_iota(jnp.int32, (nz, width), 0)
        away = peer_number // 4 + 1
        offset = jnp.where((peer_number // 2) % 2 == 0, away, jnp.where(away == half, 0, -away))
        place = chip + offset
        place = jnp.where(place < 0, place + chips, jnp.where(place >= chips, place - chips, place))
        peer = place * 2 + peer_number % 2
        table = jnp.full((nz, width), -1, jnp.int32)
        for l in range(slots):
            table = jnp.where(links[0:1, l : l + 1] == peer, index[l : l + 1, :], table)
        peer_index[...] = table

    def make_onehots(group, carry):
        for r in range(4):
            hot = hot_of(peer_index[pl.ds(group * 4 + r, 1), :])
            onehot[group, :, r * width : (r + 1) * width] = hot
            onehot_t[group, r * width : (r + 1) * width, :] = hot.T
        return carry

    def gather_and_send(x):
        stacked = jnp.concatenate(halves(x), axis=0)

        def gather_group(group):
            for r in range(4):
                departing[1, group * 4 + r] = pick_faces(
                    stacked, onehot[group, :, r * width : (r + 1) * width], peer_index[pl.ds(group * 4 + r, 1), :]
                )

        gather_group(half - 1)
        send_last(1)

        def body(t, carry):
            group = half - 2 - t
            gather_group(group)
            send_group(1, group)
            return carry

        lax.fori_loop(0, half - 1, body, 0)

    def land(buffer, sem, count):
        pltpu.make_async_copy(buffer.at[pl.ds(0, count)], buffer.at[pl.ds(0, count)], sem).wait()

    def add_group(step, group, count):
        land(arriving.at[step], recv_sems.at[step, group], count)
        chosen = chosen_of(group_row(group))
        blocks = [arriving[step, group * 4 + r] for r in range(4)]
        highs = [block.astype(bf16).astype(f32) for block in blocks]
        lows = [block - high for block, high in zip(blocks, highs)]
        spread = jnp.concatenate(
            [
                jnp.where(
                    chosen,
                    jnp.concatenate(
                        [part[j * probes + p : j * probes + p + 1] for part in parts for j in range(pieces)], axis=1
                    ),
                    0.0,
                )
                for parts in (highs, lows)
                for p in range(probes)
            ],
            axis=0,
        ).astype(bf16)
        placed[...] += nn_dot(spread, onehot_t[group])

    def receive(step):
        placed[...] = jnp.zeros_like(placed)

        def body(group, carry):
            add_group(step, group, 4)
            return carry

        lax.fori_loop(0, half - 1, body, 0)
        add_group(step, half - 1, 3)
        return placed[:rows] + placed[rows:]

    for step in range(2):
        arriving[step, (half - 1) * 4 + 2 + core] = jnp.zeros((8, LANES), f32)
    first_pre = per_element(source, p_high, p_low) * inverse_rows
    pre_one[...] = first_pre
    pltpu.make_async_copy(pre_one, pre_one_out, out_sems.at[0]).start()
    loads[0].wait()
    gather_slots(first_pre)
    fill_departing()
    pl.semaphore_wait(barrier, nz - 1 + nxy - 1)
    send_last(0)

    def send_body(t, carry):
        send_group(0, half - 2 - t)
        return carry

    lax.fori_loop(0, half - 1, send_body, 0)
    make_peer_index()
    lax.fori_loop(0, half, make_onehots, 0)
    loads[6].wait()
    k_high[...], k_low[...] = halves(k_raw[...])
    local_part = per_element(first_pre, k_high, k_low) * visc_rows
    first_img = (local_part - coupling * receive(0)) * live_rows
    second_pre = per_element(first_img, p_high, p_low) * inverse_rows
    gather_and_send(second_pre)
    pre_two[...] = second_pre
    pltpu.make_async_copy(pre_two, pre_two_out, out_sems.at[1]).start()

    lane = lax.broadcasted_iota(jnp.int32, (1, LANES), 1)

    def note(partial, q, a, b):
        product = a * b
        for p in range(probes):
            column = jnp.sum(product[p * elements : (p + 1) * elements], axis=0, keepdims=True)
            value = jnp.sum(column, axis=1, keepdims=True)
            partial = jnp.where(lane == q * probes + p, value, partial)
        return partial

    partial = jnp.zeros((1, LANES), f32)
    partial = note(partial, 0, first_img, first_img)
    partial = note(partial, 3, first_img, source)
    local_part = per_element(second_pre, k_high, k_low) * visc_rows
    second_img = (local_part - coupling * receive(1)) * live_rows
    partial = note(partial, 1, first_img, second_img)
    partial = note(partial, 2, second_img, second_img)
    partial = note(partial, 4, second_img, source)

    def all_sum(buffer, mine, count, stage, device_of, part):
        buffer[mine] = part

        def send(j, carry):
            pltpu.make_async_remote_copy(
                src_ref=buffer.at[mine],
                dst_ref=buffer.at[mine],
                send_sem=send_sems.at[2 + stage],
                recv_sem=sum_sems.at[stage],
                device_id=device_of(j),
                device_id_type=MESH,
            ).start()
            return carry

        lax.fori_loop(0, count - 1, send, 0)
        land(buffer, sum_sems.at[stage], count - 1)
        total = buffer[0]
        for s in range(1, count):
            total = total + buffer[s]
        return total

    def xy_device(j):
        other = xy_peer(j)
        return (other // ny, other % ny, me)

    total = all_sum(sums_z, me, nz, 0, lambda j: (ix, iy, z_peer(j)), partial)
    total = all_sum(sums_xy, plane, nxy, 1, xy_device, total)

    for p in range(probes):
        self_one, cross_mid, self_two, load_one, load_two = (
            jnp.sum(jnp.where(lane == q * probes + p, total, 0.0), axis=1, keepdims=True) for q in range(5)
        )
        determinant = self_one * self_two - cross_mid * cross_mid
        weight_one = (self_two * load_one - cross_mid * load_two) / determinant
        weight_two = (self_one * load_two - cross_mid * load_one) / determinant
        weights_ref[p : p + 1] = jnp.broadcast_to(weight_one, (1, LANES))
        weights_ref[probes + p : probes + p + 1] = jnp.broadcast_to(weight_two, (1, LANES))

    pltpu.make_async_copy(pre_one, pre_one_out, out_sems.at[0]).wait()
    pltpu.make_async_copy(pre_two, pre_two_out, out_sems.at[1]).wait()
    land(departing.at[0], send_sems.at[0], nz - 1)
    land(departing.at[1], send_sems.at[1], nz - 1)
    land(sums_z, send_sems.at[2], nz - 1)
    land(sums_xy, send_sems.at[3], nxy - 1)


def solution(mesh):
    nx, ny, nz = (mesh.shape[name] for name in ("gx", "gy", "gz"))

    def per_device(rhs, viscosity, counts, neighbours, face_index, k_matrix, p_matrix):
        probes, elements, dofs = rhs.shape[3:]
        slots, width = face_index.shape[3:]
        rows = probes * elements
        vmem = pltpu.VMEM
        any_space = pl.BlockSpec(memory_space=pl.ANY)
        field = jax.ShapeDtypeStruct((rows, dofs), f32)
        half = nz // 4
        first_pre, second_pre, weights = pl.pallas_call(
            functools.partial(kernel, nx, ny, nz, slots, probes, elements, dofs, width),
            out_shape=(field, field, jax.ShapeDtypeStruct((2 * probes, LANES), f32)),
            in_specs=[any_space] * 7,
            out_specs=(any_space, any_space, pl.BlockSpec(memory_space=vmem)),
            scratch_shapes=[
                vmem((rows, dofs), f32),
                vmem((1, elements), f32),
                vmem((1, 1), jnp.int32),
                vmem((1, slots), jnp.int32),
                vmem((slots, width), jnp.int32),
                vmem((dofs, dofs), f32),
                vmem((dofs, dofs), f32),
                vmem((dofs, dofs), bf16),
                vmem((dofs, dofs), bf16),
                vmem((dofs, dofs), bf16),
                vmem((dofs, dofs), bf16),
                vmem((nz, width), jnp.int32),
                vmem((half, dofs, 4 * width), bf16),
                vmem((half, 4 * width, dofs), bf16),
                vmem((slots, 8, LANES), f32),
                vmem((2, nz, 8, LANES), f32),
                vmem((2, nz, 8, LANES), f32),
                vmem((2 * rows, dofs), f32),
                vmem((rows, dofs), f32),
                vmem((rows, dofs), f32),
                vmem((nz, 1, LANES), f32),
                vmem((nx * ny, 1, LANES), f32),
                pltpu.SemaphoreType.DMA((7,)),
                pltpu.SemaphoreType.DMA((2,)),
                pltpu.SemaphoreType.DMA((4,)),
                pltpu.SemaphoreType.DMA((2, half)),
                pltpu.SemaphoreType.DMA((2,)),
            ],
            compiler_params=pltpu.CompilerParams(collective_id=0, has_side_effects=True),
        )(
            rhs.reshape(rows, dofs),
            viscosity.reshape(1, elements),
            counts.reshape(1, 1),
            neighbours.reshape(1, slots),
            face_index.reshape(slots, width),
            k_matrix,
            p_matrix,
        )
        scale_one = weights[:probes, 0][:, None, None]
        scale_two = weights[probes:, 0][:, None, None]
        shape = (probes, elements, dofs)
        out = scale_one * first_pre.reshape(shape) + scale_two * second_pre.reshape(shape)
        return out.reshape(rhs.shape)

    return jax.shard_map(
        per_device,
        mesh=mesh,
        in_specs=(
            P("gx", "gy", "gz", None, None, None),
            P("gx", "gy", "gz", None),
            P("gx", "gy", "gz"),
            P("gx", "gy", "gz", None),
            P("gx", "gy", "gz", None, None),
            P(),
            P(),
        ),
        out_specs=P("gx", "gy", "gz", None, None, None),
        check_vma=False,
    )
```

```python
import functools

import jax
import jax.numpy as jnp
from jax import lax
from jax.experimental import pallas as pl
from jax.experimental.pallas import tpu as pltpu
from jax.sharding import PartitionSpec as P

MESH = pl.DeviceIdType.MESH
coupling = 0.5
LANES = 128
f32 = jnp.float32
bf16 = jnp.bfloat16


def halves(x):
    high = x.astype(bf16)
    low = (x - high.astype(f32)).astype(bf16)
    return high, low


def nn_dot(a, b):
    return lax.dot_general(a, b, (((1,), (0,)), ((), ())), preferred_element_type=f32)


def nt_dot(a, b):
    return lax.dot_general(a, b, (((1,), (1,)), ((), ())), preferred_element_type=f32)


def kernel(
    nx, ny, nz, slots, probes, elements, dofs, width,
    rhs_hbm, visc_hbm, counts_hbm, links_hbm, index_hbm, k_hbm, p_hbm,
    out_ref,
    rhs, visc, counts, links, index, k_raw, p_raw,
    k_high, k_low, p_high, p_low, peer_index, onehot, onehot_t, faces, departing, arriving, placed,
    sums_z, sums_xy, load_sems, send_sems, recv_sems, sum_sems,
):
    ix, iy, me = lax.axis_index("gx"), lax.axis_index("gy"), lax.axis_index("gz")
    chip, core = me // 2, me % 2
    chips = nz // 2
    half = chips // 2
    nxy = nx * ny
    plane = ix * ny + iy
    rows = probes * elements
    pieces = width // LANES
    shift = dofs.bit_length() - 1

    def z_peer(j):
        offset = nz // 2 + ((j + 1) // 2) * (1 - 2 * (j % 2))
        return lax.rem(me + offset, nz)

    def xy_peer(j):
        return lax.rem(plane + 1 + j, nxy)

    def group_chip(group, side):
        away = group + 1
        offset = away if side == 0 else -away * (1 - away // half)
        return lax.rem(chip + offset + chips, chips)

    barrier = pltpu.get_barrier_semaphore()

    def greet_z(j, carry):
        pl.semaphore_signal(barrier, inc=1, device_id=(ix, iy, z_peer(j)), device_id_type=MESH)
        return carry

    def greet_xy(j, carry):
        other = xy_peer(j)
        pl.semaphore_signal(barrier, inc=1, device_id=(other // ny, other % ny, me), device_id_type=MESH)
        return carry

    loads = [
        pltpu.make_async_copy(src, dst, load_sems.at[i])
        for i, (src, dst) in enumerate(
            (
                (index_hbm, index), (rhs_hbm, rhs), (p_hbm, p_raw), (visc_hbm, visc),
                (counts_hbm, counts), (links_hbm, links), (k_hbm, k_raw),
            )
        )
    ]
    for load in loads:
        load.start()
    lax.fori_loop(0, nz - 1, greet_z, 0)
    lax.fori_loop(0, nxy - 1, greet_xy, 0)

    loads[3].wait()
    loads[4].wait()
    loads[5].wait()
    element_id = lax.broadcasted_iota(jnp.int32, (elements, 1), 0)
    live = (element_id < counts[0:1, 0:1]).astype(f32)
    diagonal = lax.broadcasted_iota(jnp.int32, (elements, elements), 0) == lax.broadcasted_iota(
        jnp.int32, (elements, elements), 1
    )
    visc_col = jnp.sum(jnp.where(diagonal, visc[0:1, :], 0.0), axis=1, keepdims=True)
    live_rows = jnp.concatenate([live] * probes, axis=0)
    visc_rows = jnp.concatenate([visc_col] * probes, axis=0)
    inverse_rows = live_rows / visc_rows

    loads[1].wait()
    loads[2].wait()
    p_high[...], p_low[...] = halves(p_raw[...])
    source = jnp.where(live_rows > 0.0, rhs[...], 0.0)

    def per_element(x, m_high, m_low):
        high, low = halves(x)
        both = nn_dot(jnp.concatenate([high, low], axis=0), m_high[...])
        return both[:rows] + both[rows:] + nn_dot(high, m_low[...])

    link_of = [jnp.broadcast_to(links[0:1, l : l + 1], (8, LANES)) for l in range(slots)]

    def hot_of(row):
        ids = lax.broadcasted_iota(jnp.int32, (dofs, row.shape[1]), 0)
        return jnp.where((row & (dofs - 1)) == ids, 1.0, 0.0).astype(bf16)

    def chosen_of(row):
        return lax.shift_right_arithmetic(row, shift) == lax.broadcasted_iota(jnp.int32, (elements, row.shape[1]), 0)

    def pick_faces(stacked, hot, row):
        spread = nn_dot(stacked, hot)
        spread = spread[:rows] + spread[rows:]
        chosen = chosen_of(row)
        picked = [
            jnp.sum(jnp.where(chosen, spread[p * elements : (p + 1) * elements], 0.0), axis=0, keepdims=True)
            for p in range(probes)
        ]
        return jnp.concatenate(
            [picked[p][:, j * LANES : (j + 1) * LANES] for j in range(pieces) for p in range(probes)], axis=0
        )

    def gather_slots(x):
        stacked = jnp.concatenate(halves(x), axis=0)

        def one_slot(l, carry):
            row = index[pl.ds(l, 1), :]
            faces[l] = pick_faces(stacked, hot_of(row), row)
            return carry

        lax.fori_loop(0, slots, one_slot, 0)

    def fill_departing():
        face_blocks = [faces[l] for l in range(slots)]

        def fill_group(group, carry):
            for side in range(2):
                for other in range(2):
                    peer = group_chip(group, side) * 2 + other
                    block = jnp.zeros((8, LANES), f32)
                    for l in range(slots):
                        block = jnp.where(link_of[l] == peer, face_blocks[l], block)
                    departing[0, group * 4 + side * 2 + other] = block
            return carry

        lax.fori_loop(0, half, fill_group, 0)

    def send_one(step, group, side, other, landing_side, box=None):
        pltpu.make_async_remote_copy(
            src_ref=departing.at[step, group * 4 + side * 2 + other],
            dst_ref=arriving.at[step, group * 4 + landing_side * 2 + core],
            send_sem=send_sems.at[step],
            recv_sem=recv_sems.at[step, group if box is None else box],
            device_id=(ix, iy, group_chip(group, side) * 2 + other),
            device_id_type=MESH,
        ).start()

    def send_far(step, other):
        send_one(step, half - 1, 0, other, 0)

    def send_twin(step):
        send_one(step, half - 1, 1, 1 - core, 1, half)

    def send_group(step, group):
        for side in range(2):
            for other in range(2):
                send_one(step, group, side, other, 1 - side)

    def make_peer_index():
        peer_number = lax.broadcasted_iota(jnp.int32, (nz, width), 0)
        away = peer_number // 4 + 1
        offset = jnp.where((peer_number // 2) % 2 == 0, away, jnp.where(away == half, 0, -away))
        place = chip + offset
        place = jnp.where(place < 0, place + chips, jnp.where(place >= chips, place - chips, place))
        peer = place * 2 + peer_number % 2
        table = jnp.full((nz, width), -1, jnp.int32)
        for l in range(slots):
            table = jnp.where(links[0:1, l : l + 1] == peer, index[l : l + 1, :], table)
        peer_index[...] = table

    def make_onehots(group, carry):
        for r in range(4):
            hot = hot_of(peer_index[pl.ds(group * 4 + r, 1), :])
            onehot[group, :, r * width : (r + 1) * width] = hot
            onehot_t[group, r * width : (r + 1) * width, :] = hot.T
        return carry

    def gather_and_send(x):
        stacked = jnp.concatenate(halves(x), axis=0)

        def gather_one(slot, group, r):
            departing[1, slot] = pick_faces(
                stacked, onehot[group, :, r * width : (r + 1) * width], peer_index[pl.ds(slot, 1), :]
            )

        for other in range(2):
            gather_one((half - 1) * 4 + other, half - 1, other)
            send_far(1, other)

        def body(t, carry):
            group = half - 2 - t
            for side in range(2):
                for other in range(2):
                    gather_one(group * 4 + side * 2 + other, group, side * 2 + other)
            send_group(1, group)
            return carry

        lax.fori_loop(0, half - 1, body, 0)
        for other in range(2):
            gather_one((half - 1) * 4 + 2 + other, half - 1, 2 + other)
        send_twin(1)

    def land(buffer, sem, count):
        pltpu.make_async_copy(buffer.at[pl.ds(0, count)], buffer.at[pl.ds(0, count)], sem).wait()

    def addend(step, group, first, count):
        row = jnp.concatenate([peer_index[pl.ds(group * 4 + r, 1), :] for r in range(first, first + count)], axis=1)
        chosen = chosen_of(row)
        blocks = [arriving[step, group * 4 + r] for r in range(first, first + count)]
        highs = [block.astype(bf16).astype(f32) for block in blocks]
        lows = [block - high for block, high in zip(blocks, highs)]
        spread = jnp.concatenate(
            [
                jnp.where(
                    chosen,
                    jnp.concatenate(
                        [part[j * probes + p : j * probes + p + 1] for part in parts for j in range(pieces)], axis=1
                    ),
                    0.0,
                )
                for parts in (highs, lows)
                for p in range(probes)
            ],
            axis=0,
        ).astype(bf16)
        return nn_dot(spread, onehot_t[group, first * width : (first + count) * width, :])

    def receive(step):
        land(arriving.at[step], recv_sems.at[step, half], 1)
        placed[...] = addend(step, half - 1, 2, 2)

        def body(group, carry):
            land(arriving.at[step], recv_sems.at[step, group], 4)
            placed[...] += addend(step, group, 0, 4)
            return carry

        lax.fori_loop(0, half - 1, body, 0)
        land(arriving.at[step], recv_sems.at[step, half - 1], 2)
        total = placed[...] + addend(step, half - 1, 0, 2)
        return total[:rows] + total[rows:]

    for step in range(2):
        arriving[step, (half - 1) * 4 + 2 + core] = jnp.zeros((8, LANES), f32)
    first_pre = per_element(source, p_high, p_low) * inverse_rows
    loads[0].wait()
    gather_slots(first_pre)
    fill_departing()
    pl.semaphore_wait(barrier, nz - 1 + nxy - 1)
    send_far(0, 0)
    send_far(0, 1)

    def send_body(t, carry):
        send_group(0, half - 2 - t)
        return carry

    lax.fori_loop(0, half - 1, send_body, 0)
    send_twin(0)
    make_peer_index()
    lax.fori_loop(0, half, make_onehots, 0)
    loads[6].wait()
    k_high[...], k_low[...] = halves(k_raw[...])
    local_part = per_element(first_pre, k_high, k_low) * visc_rows
    first_img = (local_part - coupling * receive(0)) * live_rows
    second_pre = per_element(first_img, p_high, p_low) * inverse_rows
    gather_and_send(second_pre)

    lane = lax.broadcasted_iota(jnp.int32, (1, LANES), 1)

    def note(partial, q, a, b):
        product = a * b
        for p in range(probes):
            column = jnp.sum(product[p * elements : (p + 1) * elements], axis=0, keepdims=True)
            value = jnp.sum(column, axis=1, keepdims=True)
            partial = jnp.where(lane == q * probes + p, value, partial)
        return partial

    partial = jnp.zeros((1, LANES), f32)
    partial = note(partial, 0, first_img, first_img)
    partial = note(partial, 3, first_img, source)
    local_part = per_element(second_pre, k_high, k_low) * visc_rows
    second_img = (local_part - coupling * receive(1)) * live_rows
    partial = note(partial, 1, first_img, second_img)
    partial = note(partial, 2, second_img, second_img)
    partial = note(partial, 4, second_img, source)

    def all_sum(buffer, mine, count, stage, device_of, part):
        buffer[mine] = part

        def send(j, carry):
            pltpu.make_async_remote_copy(
                src_ref=buffer.at[mine],
                dst_ref=buffer.at[mine],
                send_sem=send_sems.at[2 + stage],
                recv_sem=sum_sems.at[stage],
                device_id=device_of(j),
                device_id_type=MESH,
            ).start()
            return carry

        lax.fori_loop(0, count - 1, send, 0)
        land(buffer, sum_sems.at[stage], count - 1)
        total = buffer[0]
        for s in range(1, count):
            total = total + buffer[s]
        return total

    def xy_device(j):
        other = xy_peer(j)
        return (other // ny, other % ny, me)

    total = all_sum(sums_z, me, nz, 0, lambda j: (ix, iy, z_peer(j)), partial)
    total = all_sum(sums_xy, plane, nxy, 1, xy_device, total)

    for p in range(probes):
        self_one, cross_mid, self_two, load_one, load_two = (
            jnp.sum(jnp.where(lane == q * probes + p, total, 0.0), axis=1, keepdims=True) for q in range(5)
        )
        determinant = self_one * self_two - cross_mid * cross_mid
        weight_one = (self_two * load_one - cross_mid * load_two) / determinant
        weight_two = (self_one * load_two - cross_mid * load_one) / determinant
        part = slice(p * elements, (p + 1) * elements)
        out_ref[part] = weight_one * first_pre[part] + weight_two * second_pre[part]

    land(departing.at[0], send_sems.at[0], nz - 1)
    land(departing.at[1], send_sems.at[1], nz - 1)
    land(sums_z, send_sems.at[2], nz - 1)
    land(sums_xy, send_sems.at[3], nxy - 1)


def solution(mesh):
    nx, ny, nz = (mesh.shape[name] for name in ("gx", "gy", "gz"))

    def per_device(rhs, viscosity, counts, neighbours, face_index, k_matrix, p_matrix):
        probes, elements, dofs = rhs.shape[3:]
        slots, width = face_index.shape[3:]
        rows = probes * elements
        vmem = pltpu.VMEM
        stay = functools.partial(pltpu.with_memory_space_constraint, memory_space=pltpu.HBM)
        hbm = pl.BlockSpec(memory_space=pltpu.HBM)
        half = nz // 4
        out = pl.pallas_call(
            functools.partial(kernel, nx, ny, nz, slots, probes, elements, dofs, width),
            out_shape=jax.ShapeDtypeStruct((rows, dofs), f32),
            in_specs=[hbm] * 7,
            out_specs=pl.BlockSpec(memory_space=vmem),
            scratch_shapes=[
                vmem((rows, dofs), f32),
                vmem((1, elements), f32),
                vmem((1, 1), jnp.int32),
                vmem((1, slots), jnp.int32),
                vmem((slots, width), jnp.int32),
                vmem((dofs, dofs), f32),
                vmem((dofs, dofs), f32),
                vmem((dofs, dofs), bf16),
                vmem((dofs, dofs), bf16),
                vmem((dofs, dofs), bf16),
                vmem((dofs, dofs), bf16),
                vmem((nz, width), jnp.int32),
                vmem((half, dofs, 4 * width), bf16),
                vmem((half, 4 * width, dofs), bf16),
                vmem((slots, 8, LANES), f32),
                vmem((2, nz, 8, LANES), f32),
                vmem((2, nz, 8, LANES), f32),
                vmem((2 * rows, dofs), f32),
                vmem((nz, 1, LANES), f32),
                vmem((nx * ny, 1, LANES), f32),
                pltpu.SemaphoreType.DMA((7,)),
                pltpu.SemaphoreType.DMA((4,)),
                pltpu.SemaphoreType.DMA((2, half + 1)),
                pltpu.SemaphoreType.DMA((2,)),
            ],
            compiler_params=pltpu.CompilerParams(collective_id=0, has_side_effects=True, vmem_limit_bytes=24 * 1024 * 1024),
        )(
            stay(rhs.reshape(rows, dofs)),
            stay(viscosity.reshape(1, elements)),
            counts.reshape(1, 1),
            stay(neighbours.reshape(1, slots)),
            stay(face_index.reshape(slots, width)),
            stay(k_matrix),
            stay(p_matrix),
        )
        return out.reshape(rhs.shape)

    return jax.shard_map(
        per_device,
        mesh=mesh,
        in_specs=(
            P("gx", "gy", "gz", None, None, None),
            P("gx", "gy", "gz", None),
            P("gx", "gy", "gz"),
            P("gx", "gy", "gz", None),
            P("gx", "gy", "gz", None, None),
            P(),
            P(),
        ),
        out_specs=P("gx", "gy", "gz", None, None, None),
        check_vma=False,
    )
```

```python
import functools

import jax
import jax.numpy as jnp
from jax import lax
from jax.experimental import pallas as pl
from jax.experimental.pallas import tpu as pltpu
from jax.sharding import PartitionSpec as P

MESH = pl.DeviceIdType.MESH
coupling = 0.5
LANES = 128
f32 = jnp.float32
bf16 = jnp.bfloat16


def halves(x):
    high = x.astype(bf16)
    low = (x - high.astype(f32)).astype(bf16)
    return high, low


def nn_dot(a, b):
    return lax.dot_general(a, b, (((1,), (0,)), ((), ())), preferred_element_type=f32)


def nt_dot(a, b):
    return lax.dot_general(a, b, (((1,), (1,)), ((), ())), preferred_element_type=f32)


def kernel(
    nx, ny, nz, slots, probes, elements, dofs, width,
    rhs_hbm, visc_hbm, counts_hbm, links_hbm, index_hbm, k_hbm, p_hbm,
    out_ref,
    rhs, visc, counts, links, index, k_raw, p_raw,
    k_high, k_low, p_high, p_low, peer_index, onehot, onehot_t, faces, departing, arriving, placed,
    sums_z, sums_xy, load_sems, send_sems, recv_sems, sum_sems,
):
    ix, iy, me = lax.axis_index("gx"), lax.axis_index("gy"), lax.axis_index("gz")
    chip, core = me // 2, me % 2
    chips = nz // 2
    half = chips // 2
    nxy = nx * ny
    plane = ix * ny + iy
    rows = probes * elements
    pieces = width // LANES
    shift = dofs.bit_length() - 1

    def z_peer(j):
        offset = nz // 2 + ((j + 1) // 2) * (1 - 2 * (j % 2))
        return lax.rem(me + offset, nz)

    def xy_peer(j):
        across = nx // 2 + ((j // ny + 1) // 2) * (1 - 2 * ((j // ny) % 2))
        along = ny // 2 + ((j % ny + 1) // 2) * (1 - 2 * ((j % ny) % 2))
        return lax.rem(ix + across, nx) * ny + lax.rem(iy + along, ny)

    def group_chip(group, side):
        away = group + 1
        offset = away if side == 0 else -away * (1 - away // half)
        return lax.rem(chip + offset + chips, chips)

    barrier = pltpu.get_barrier_semaphore()

    def greet_z(j, carry):
        pl.semaphore_signal(barrier, inc=1, device_id=(ix, iy, z_peer(j)), device_id_type=MESH)
        return carry

    def greet_xy(j, carry):
        other = xy_peer(j)
        pl.semaphore_signal(barrier, inc=1, device_id=(other // ny, other % ny, me), device_id_type=MESH)
        return carry

    loads = [
        pltpu.make_async_copy(src, dst, load_sems.at[i])
        for i, (src, dst) in enumerate(
            (
                (index_hbm, index), (rhs_hbm, rhs), (p_hbm, p_raw), (visc_hbm, visc),
                (counts_hbm, counts), (links_hbm, links), (k_hbm, k_raw),
            )
        )
    ]
    for load in loads:
        load.start()
    lax.fori_loop(0, nz - 1, greet_z, 0)
    lax.fori_loop(0, nxy - 1, greet_xy, 0)

    loads[3].wait()
    loads[4].wait()
    loads[5].wait()
    element_id = lax.broadcasted_iota(jnp.int32, (elements, 1), 0)
    live = (element_id < counts[0:1, 0:1]).astype(f32)
    diagonal = lax.broadcasted_iota(jnp.int32, (elements, elements), 0) == lax.broadcasted_iota(
        jnp.int32, (elements, elements), 1
    )
    visc_col = jnp.sum(jnp.where(diagonal, visc[0:1, :], 0.0), axis=1, keepdims=True)
    live_rows = jnp.concatenate([live] * probes, axis=0)
    visc_rows = jnp.concatenate([visc_col] * probes, axis=0)
    inverse_rows = live_rows / visc_rows

    loads[1].wait()
    loads[2].wait()
    p_high[...], p_low[...] = halves(p_raw[...])
    source = jnp.where(live_rows > 0.0, rhs[...], 0.0)

    def per_element(x, m_high, m_low):
        high, low = halves(x)
        both = nn_dot(jnp.concatenate([high, low], axis=0), m_high[...])
        return both[:rows] + both[rows:] + nn_dot(high, m_low[...])

    link_of = [jnp.broadcast_to(links[0:1, l : l + 1], (8, LANES)) for l in range(slots)]

    def hot_of(row):
        ids = lax.broadcasted_iota(jnp.int32, (dofs, row.shape[1]), 0)
        return jnp.where((row & (dofs - 1)) == ids, 1.0, 0.0).astype(bf16)

    def chosen_of(row):
        return lax.shift_right_arithmetic(row, shift) == lax.broadcasted_iota(jnp.int32, (elements, row.shape[1]), 0)

    def pick_faces(stacked, hot, row):
        spread = nn_dot(stacked, hot)
        spread = spread[:rows] + spread[rows:]
        chosen = chosen_of(row)
        picked = [
            jnp.sum(jnp.where(chosen, spread[p * elements : (p + 1) * elements], 0.0), axis=0, keepdims=True)
            for p in range(probes)
        ]
        return jnp.concatenate(
            [picked[p][:, j * LANES : (j + 1) * LANES] for j in range(pieces) for p in range(probes)], axis=0
        )

    def gather_slots(x):
        stacked = jnp.concatenate(halves(x), axis=0)

        def one_slot(l, carry):
            row = index[pl.ds(l, 1), :]
            faces[l] = pick_faces(stacked, hot_of(row), row)
            return carry

        lax.fori_loop(0, slots, one_slot, 0)

    def fill_departing():
        face_blocks = [faces[l] for l in range(slots)]

        def fill_group(group, carry):
            for side in range(2):
                for other in range(2):
                    peer = group_chip(group, side) * 2 + other
                    block = jnp.zeros((8, LANES), f32)
                    for l in range(slots):
                        block = jnp.where(link_of[l] == peer, face_blocks[l], block)
                    departing[0, group * 4 + side * 2 + other] = block
            return carry

        lax.fori_loop(0, half, fill_group, 0)

    def send_one(step, group, side, other, landing_side, box=None):
        pltpu.make_async_remote_copy(
            src_ref=departing.at[step, group * 4 + side * 2 + other],
            dst_ref=arriving.at[step, group * 4 + landing_side * 2 + core],
            send_sem=send_sems.at[step],
            recv_sem=recv_sems.at[step, group if box is None else box],
            device_id=(ix, iy, group_chip(group, side) * 2 + other),
            device_id_type=MESH,
        ).start()

    def send_far(step, other):
        send_one(step, half - 1, 0, other, 0)

    def send_twin(step):
        send_one(step, half - 1, 1, 1 - core, 1, half)

    def send_group(step, group):
        for side in range(2):
            for other in range(2):
                send_one(step, group, side, other, 1 - side)

    def make_peer_index():
        peer_number = lax.broadcasted_iota(jnp.int32, (nz, width), 0)
        away = peer_number // 4 + 1
        offset = jnp.where((peer_number // 2) % 2 == 0, away, jnp.where(away == half, 0, -away))
        place = chip + offset
        place = jnp.where(place < 0, place + chips, jnp.where(place >= chips, place - chips, place))
        peer = place * 2 + peer_number % 2
        table = jnp.full((nz, width), -1, jnp.int32)
        for l in range(slots):
            table = jnp.where(links[0:1, l : l + 1] == peer, index[l : l + 1, :], table)
        peer_index[...] = table

    def make_onehots(group, carry):
        for r in range(4):
            hot = hot_of(peer_index[pl.ds(group * 4 + r, 1), :])
            onehot[group, :, r * width : (r + 1) * width] = hot
            onehot_t[group, r * width : (r + 1) * width, :] = hot.T
        return carry

    def gather_and_send(x):
        stacked = jnp.concatenate(halves(x), axis=0)

        def gather_one(slot, group, r):
            departing[1, slot] = pick_faces(
                stacked, onehot[group, :, r * width : (r + 1) * width], peer_index[pl.ds(slot, 1), :]
            )

        for other in range(2):
            gather_one((half - 1) * 4 + other, half - 1, other)
            send_far(1, other)

        def body(t, carry):
            group = half - 2 - t
            for side in range(2):
                for other in range(2):
                    gather_one(group * 4 + side * 2 + other, group, side * 2 + other)
            send_group(1, group)
            return carry

        lax.fori_loop(0, half - 1, body, 0)
        for other in range(2):
            gather_one((half - 1) * 4 + 2 + other, half - 1, 2 + other)
        send_twin(1)

    def land(buffer, sem, count):
        pltpu.make_async_copy(buffer.at[pl.ds(0, count)], buffer.at[pl.ds(0, count)], sem).wait()

    def addend(step, group, first, count):
        row = jnp.concatenate([peer_index[pl.ds(group * 4 + r, 1), :] for r in range(first, first + count)], axis=1)
        chosen = chosen_of(row)
        blocks = [arriving[step, group * 4 + r] for r in range(first, first + count)]
        highs = [block.astype(bf16).astype(f32) for block in blocks]
        lows = [block - high for block, high in zip(blocks, highs)]
        spread = jnp.concatenate(
            [
                jnp.where(
                    chosen,
                    jnp.concatenate(
                        [part[j * probes + p : j * probes + p + 1] for part in parts for j in range(pieces)], axis=1
                    ),
                    0.0,
                )
                for parts in (highs, lows)
                for p in range(probes)
            ],
            axis=0,
        ).astype(bf16)
        return nn_dot(spread, onehot_t[group, first * width : (first + count) * width, :])

    def receive(step):
        land(arriving.at[step], recv_sems.at[step, half], 1)
        placed[...] = addend(step, half - 1, 2, 2)

        def body(group, carry):
            land(arriving.at[step], recv_sems.at[step, group], 4)
            placed[...] += addend(step, group, 0, 4)
            return carry

        lax.fori_loop(0, half - 1, body, 0)
        land(arriving.at[step], recv_sems.at[step, half - 1], 2)
        total = placed[...] + addend(step, half - 1, 0, 2)
        return total[:rows] + total[rows:]

    for step in range(2):
        arriving[step, (half - 1) * 4 + 2 + core] = jnp.zeros((8, LANES), f32)
    first_pre = per_element(source, p_high, p_low) * inverse_rows
    loads[0].wait()
    gather_slots(first_pre)
    fill_departing()
    pl.semaphore_wait(barrier, nz - 1 + nxy - 1)
    send_far(0, 0)
    send_far(0, 1)

    def send_body(t, carry):
        send_group(0, half - 2 - t)
        return carry

    lax.fori_loop(0, half - 1, send_body, 0)
    send_twin(0)
    make_peer_index()
    lax.fori_loop(0, half, make_onehots, 0)
    loads[6].wait()
    k_high[...], k_low[...] = halves(k_raw[...])
    local_part = per_element(first_pre, k_high, k_low) * visc_rows
    first_img = (local_part - coupling * receive(0)) * live_rows
    second_pre = per_element(first_img, p_high, p_low) * inverse_rows
    gather_and_send(second_pre)

    lane = lax.broadcasted_iota(jnp.int32, (1, LANES), 1)

    def note(partial, q, a, b):
        product = a * b
        for p in range(probes):
            column = jnp.sum(product[p * elements : (p + 1) * elements], axis=0, keepdims=True)
            value = jnp.sum(column, axis=1, keepdims=True)
            partial = jnp.where(lane == q * probes + p, value, partial)
        return partial

    partial = jnp.zeros((1, LANES), f32)
    partial = note(partial, 0, first_img, first_img)
    partial = note(partial, 3, first_img, source)
    local_part = per_element(second_pre, k_high, k_low) * visc_rows
    second_img = (local_part - coupling * receive(1)) * live_rows
    partial = note(partial, 1, first_img, second_img)
    partial = note(partial, 2, second_img, second_img)
    partial = note(partial, 4, second_img, source)

    def all_sum(buffer, mine, count, stage, device_of, part):
        buffer[mine] = part

        def send(j, carry):
            pltpu.make_async_remote_copy(
                src_ref=buffer.at[mine],
                dst_ref=buffer.at[mine],
                send_sem=send_sems.at[2 + stage],
                recv_sem=sum_sems.at[stage],
                device_id=device_of(j),
                device_id_type=MESH,
            ).start()
            return carry

        lax.fori_loop(0, count - 1, send, 0)
        land(buffer, sum_sems.at[stage], count - 1)
        total = buffer[0]
        for s in range(1, count):
            total = total + buffer[s]
        return total

    def xy_device(j):
        other = xy_peer(j)
        return (other // ny, other % ny, me)

    total = all_sum(sums_z, me, nz, 0, lambda j: (ix, iy, z_peer(j)), partial)
    total = all_sum(sums_xy, plane, nxy, 1, xy_device, total)

    for p in range(probes):
        self_one, cross_mid, self_two, load_one, load_two = (
            jnp.sum(jnp.where(lane == q * probes + p, total, 0.0), axis=1, keepdims=True) for q in range(5)
        )
        determinant = self_one * self_two - cross_mid * cross_mid
        weight_one = (self_two * load_one - cross_mid * load_two) / determinant
        weight_two = (self_one * load_two - cross_mid * load_one) / determinant
        part = slice(p * elements, (p + 1) * elements)
        out_ref[part] = weight_one * first_pre[part] + weight_two * second_pre[part]

    land(departing.at[0], send_sems.at[0], nz - 1)
    land(departing.at[1], send_sems.at[1], nz - 1)
    land(sums_z, send_sems.at[2], nz - 1)
    land(sums_xy, send_sems.at[3], nxy - 1)


def solution(mesh):
    nx, ny, nz = (mesh.shape[name] for name in ("gx", "gy", "gz"))

    def per_device(rhs, viscosity, counts, neighbours, face_index, k_matrix, p_matrix):
        probes, elements, dofs = rhs.shape[3:]
        slots, width = face_index.shape[3:]
        rows = probes * elements
        vmem = pltpu.VMEM
        stay = functools.partial(pltpu.with_memory_space_constraint, memory_space=pltpu.HBM)
        hbm = pl.BlockSpec(memory_space=pltpu.HBM)
        half = nz // 4
        out = pl.pallas_call(
            functools.partial(kernel, nx, ny, nz, slots, probes, elements, dofs, width),
            out_shape=jax.ShapeDtypeStruct((rows, dofs), f32),
            in_specs=[hbm] * 7,
            out_specs=pl.BlockSpec(memory_space=vmem),
            scratch_shapes=[
                vmem((rows, dofs), f32),
                vmem((1, elements), f32),
                vmem((1, 1), jnp.int32),
                vmem((1, slots), jnp.int32),
                vmem((slots, width), jnp.int32),
                vmem((dofs, dofs), f32),
                vmem((dofs, dofs), f32),
                vmem((dofs, dofs), bf16),
                vmem((dofs, dofs), bf16),
                vmem((dofs, dofs), bf16),
                vmem((dofs, dofs), bf16),
                vmem((nz, width), jnp.int32),
                vmem((half, dofs, 4 * width), bf16),
                vmem((half, 4 * width, dofs), bf16),
                vmem((slots, 8, LANES), f32),
                vmem((2, nz, 8, LANES), f32),
                vmem((2, nz, 8, LANES), f32),
                vmem((2 * rows, dofs), f32),
                vmem((nz, 1, LANES), f32),
                vmem((nx * ny, 1, LANES), f32),
                pltpu.SemaphoreType.DMA((7,)),
                pltpu.SemaphoreType.DMA((4,)),
                pltpu.SemaphoreType.DMA((2, half + 1)),
                pltpu.SemaphoreType.DMA((2,)),
            ],
            compiler_params=pltpu.CompilerParams(collective_id=0, has_side_effects=True, vmem_limit_bytes=24 * 1024 * 1024),
        )(
            stay(rhs.reshape(rows, dofs)),
            stay(viscosity.reshape(1, elements)),
            counts.reshape(1, 1),
            stay(neighbours.reshape(1, slots)),
            stay(face_index.reshape(slots, width)),
            stay(k_matrix),
            stay(p_matrix),
        )
        return out.reshape(rhs.shape)

    return jax.shard_map(
        per_device,
        mesh=mesh,
        in_specs=(
            P("gx", "gy", "gz", None, None, None),
            P("gx", "gy", "gz", None),
            P("gx", "gy", "gz"),
            P("gx", "gy", "gz", None),
            P("gx", "gy", "gz", None, None),
            P(),
            P(),
        ),
        out_specs=P("gx", "gy", "gz", None, None, None),
        check_vma=False,
    )
```

```python
import functools

import jax
import jax.numpy as jnp
from jax import lax
from jax.experimental import pallas as pl
from jax.experimental.pallas import tpu as pltpu
from jax.sharding import PartitionSpec as P

MESH = pl.DeviceIdType.MESH
coupling = 0.5
LANES = 128
f32 = jnp.float32
bf16 = jnp.bfloat16


def halves(x):
    high = x.astype(bf16)
    low = (x - high.astype(f32)).astype(bf16)
    return high, low


def nn_dot(a, b):
    return lax.dot_general(a, b, (((1,), (0,)), ((), ())), preferred_element_type=f32)


def nt_dot(a, b):
    return lax.dot_general(a, b, (((1,), (1,)), ((), ())), preferred_element_type=f32)


def kernel(
    nx, ny, nz, slots, probes, elements, dofs, width,
    rhs_hbm, visc_hbm, counts_hbm, links_hbm, index_hbm, k_hbm, p_hbm,
    out_ref,
    rhs, visc, counts, links, index, k_raw, p_raw,
    k_high, k_low, p_high, p_low, peer_index, onehot, onehot_t, faces, departing, arriving, placed,
    sums_z, sums_xy, load_sems, send_sems, recv_sems, sum_sems,
):
    ix, iy, me = lax.axis_index("gx"), lax.axis_index("gy"), lax.axis_index("gz")
    chip, core = me // 2, me % 2
    chips = nz // 2
    half = chips // 2
    nxy = nx * ny
    plane = ix * ny + iy
    rows = probes * elements
    pieces = width // LANES
    shift = dofs.bit_length() - 1

    def z_peer(j):
        offset = nz // 2 + ((j + 1) // 2) * (1 - 2 * (j % 2))
        return lax.rem(me + offset, nz)

    def xy_peer(j):
        across = nx // 2 + ((j // ny + 1) // 2) * (1 - 2 * ((j // ny) % 2))
        along = ny // 2 + ((j % ny + 1) // 2) * (1 - 2 * ((j % ny) % 2))
        return lax.rem(ix + across, nx) * ny + lax.rem(iy + along, ny)

    def group_chip(group, side):
        away = group + 1
        offset = away if side == 0 else -away * (1 - away // half)
        return lax.rem(chip + offset + chips, chips)

    barrier = pltpu.get_barrier_semaphore()

    def greet_z(j, carry):
        pl.semaphore_signal(barrier, inc=1, device_id=(ix, iy, z_peer(j)), device_id_type=MESH)
        return carry

    def greet_xy(j, carry):
        other = xy_peer(j)
        pl.semaphore_signal(barrier, inc=1, device_id=(other // ny, other % ny, me), device_id_type=MESH)
        return carry

    loads = [
        pltpu.make_async_copy(src, dst, load_sems.at[i])
        for i, (src, dst) in enumerate(
            (
                (index_hbm, index), (rhs_hbm, rhs), (p_hbm, p_raw), (visc_hbm, visc),
                (counts_hbm, counts), (links_hbm, links), (k_hbm, k_raw),
            )
        )
    ]
    for load in loads:
        load.start()
    lax.fori_loop(0, nz - 1, greet_z, 0)
    lax.fori_loop(0, nxy - 1, greet_xy, 0)

    loads[3].wait()
    loads[4].wait()
    loads[5].wait()
    element_id = lax.broadcasted_iota(jnp.int32, (elements, 1), 0)
    live = (element_id < counts[0:1, 0:1]).astype(f32)
    diagonal = lax.broadcasted_iota(jnp.int32, (elements, elements), 0) == lax.broadcasted_iota(
        jnp.int32, (elements, elements), 1
    )
    visc_col = jnp.sum(jnp.where(diagonal, visc[0:1, :], 0.0), axis=1, keepdims=True)
    live_rows = jnp.concatenate([live] * probes, axis=0)
    visc_rows = jnp.concatenate([visc_col] * probes, axis=0)
    inverse_rows = live_rows / visc_rows

    loads[1].wait()
    loads[2].wait()
    p_high[...], p_low[...] = halves(p_raw[...])
    source = jnp.where(live_rows > 0.0, rhs[...], 0.0)

    def per_element(x, m_high, m_low):
        high, low = halves(x)
        both = nn_dot(jnp.concatenate([high, low], axis=0), m_high[...])
        return both[:rows] + both[rows:] + nn_dot(high, m_low[...])

    link_of = [jnp.broadcast_to(links[0:1, l : l + 1], (8, LANES)) for l in range(slots)]

    def hot_of(row):
        ids = lax.broadcasted_iota(jnp.int32, (dofs, row.shape[1]), 0)
        return jnp.where((row & (dofs - 1)) == ids, 1.0, 0.0).astype(bf16)

    def chosen_of(row):
        return lax.shift_right_arithmetic(row, shift) == lax.broadcasted_iota(jnp.int32, (elements, row.shape[1]), 0)

    def pick_faces(stacked, hot, row):
        spread = nn_dot(stacked, hot)
        spread = spread[:rows] + spread[rows:]
        chosen = chosen_of(row)
        picked = [
            jnp.sum(jnp.where(chosen, spread[p * elements : (p + 1) * elements], 0.0), axis=0, keepdims=True)
            for p in range(probes)
        ]
        return jnp.concatenate(
            [picked[p][:, j * LANES : (j + 1) * LANES] for j in range(pieces) for p in range(probes)], axis=0
        )

    def gather_slots(x):
        stacked = jnp.concatenate(halves(x), axis=0)

        def one_slot(l, carry):
            row = index[pl.ds(l, 1), :]
            faces[l] = pick_faces(stacked, hot_of(row), row)
            return carry

        lax.fori_loop(0, slots, one_slot, 0)

    def fill_departing():
        face_blocks = [faces[l] for l in range(slots)]

        def fill_group(group, carry):
            for side in range(2):
                for other in range(2):
                    peer = group_chip(group, side) * 2 + other
                    block = jnp.zeros((8, LANES), f32)
                    for l in range(slots):
                        block = jnp.where(link_of[l] == peer, face_blocks[l], block)
                    departing[0, group * 4 + side * 2 + other] = block
            return carry

        lax.fori_loop(0, half, fill_group, 0)

    def send_one(step, group, side, other, landing_side, box=None):
        pltpu.make_async_remote_copy(
            src_ref=departing.at[step, group * 4 + side * 2 + other],
            dst_ref=arriving.at[step, group * 4 + landing_side * 2 + core],
            send_sem=send_sems.at[step],
            recv_sem=recv_sems.at[step, group if box is None else box],
            device_id=(ix, iy, group_chip(group, side) * 2 + other),
            device_id_type=MESH,
        ).start()

    def send_far(step, other):
        send_one(step, half - 1, 0, other, 0)

    def send_twin(step):
        send_one(step, half - 1, 1, 1 - core, 1, half)

    def send_group(step, group):
        for side in range(2):
            for other in range(2):
                send_one(step, group, side, other, 1 - side)

    def make_peer_index():
        peer_number = lax.broadcasted_iota(jnp.int32, (nz, width), 0)
        away = peer_number // 4 + 1
        offset = jnp.where((peer_number // 2) % 2 == 0, away, jnp.where(away == half, 0, -away))
        place = chip + offset
        place = jnp.where(place < 0, place + chips, jnp.where(place >= chips, place - chips, place))
        peer = place * 2 + peer_number % 2
        table = jnp.full((nz, width), -1, jnp.int32)
        for l in range(slots):
            table = jnp.where(links[0:1, l : l + 1] == peer, index[l : l + 1, :], table)
        peer_index[...] = table

    def make_onehots(group, carry):
        for r in range(4):
            hot = hot_of(peer_index[pl.ds(group * 4 + r, 1), :])
            onehot[group, :, r * width : (r + 1) * width] = hot
            onehot_t[group, r * width : (r + 1) * width, :] = hot.T
        return carry

    def gather_and_send(x):
        stacked = jnp.concatenate(halves(x), axis=0)

        def gather_one(slot, group, r):
            departing[1, slot] = pick_faces(
                stacked, onehot[group, :, r * width : (r + 1) * width], peer_index[pl.ds(slot, 1), :]
            )

        for other in range(2):
            gather_one((half - 1) * 4 + other, half - 1, other)
            send_far(1, other)

        def body(t, carry):
            group = half - 2 - t
            for side in range(2):
                for other in range(2):
                    gather_one(group * 4 + side * 2 + other, group, side * 2 + other)
            send_group(1, group)
            return carry

        lax.fori_loop(0, half - 1, body, 0)
        for other in range(2):
            gather_one((half - 1) * 4 + 2 + other, half - 1, 2 + other)
        send_twin(1)

    def land(buffer, sem, count):
        pltpu.make_async_copy(buffer.at[pl.ds(0, count)], buffer.at[pl.ds(0, count)], sem).wait()

    def addend(step, group, first, count):
        row = jnp.concatenate([peer_index[pl.ds(group * 4 + r, 1), :] for r in range(first, first + count)], axis=1)
        chosen = chosen_of(row)
        blocks = [arriving[step, group * 4 + r] for r in range(first, first + count)]
        highs = [block.astype(bf16).astype(f32) for block in blocks]
        lows = [block - high for block, high in zip(blocks, highs)]
        spread = jnp.concatenate(
            [
                jnp.where(
                    chosen,
                    jnp.concatenate(
                        [part[j * probes + p : j * probes + p + 1] for part in parts for j in range(pieces)], axis=1
                    ),
                    0.0,
                )
                for parts in (highs, lows)
                for p in range(probes)
            ],
            axis=0,
        ).astype(bf16)
        return nn_dot(spread, onehot_t[group, first * width : (first + count) * width, :])

    def receive(step):
        land(arriving.at[step], recv_sems.at[step, half], 1)
        placed[...] = addend(step, half - 1, 2, 2)

        def body(group, carry):
            land(arriving.at[step], recv_sems.at[step, group], 4)
            placed[...] += addend(step, group, 0, 4)
            return carry

        lax.fori_loop(0, half - 1, body, 0)
        land(arriving.at[step], recv_sems.at[step, half - 1], 2)
        total = placed[...] + addend(step, half - 1, 0, 2)
        return total[:rows] + total[rows:]

    for step in range(2):
        arriving[step, (half - 1) * 4 + 2 + core] = jnp.zeros((8, LANES), f32)
    first_pre = per_element(source, p_high, p_low) * inverse_rows
    loads[0].wait()
    gather_slots(first_pre)
    fill_departing()
    pl.semaphore_wait(barrier, nz - 1 + nxy - 1)
    send_far(0, 0)
    send_far(0, 1)

    def send_body(t, carry):
        send_group(0, half - 2 - t)
        return carry

    lax.fori_loop(0, half - 1, send_body, 0)
    send_twin(0)
    make_peer_index()
    lax.fori_loop(0, half, make_onehots, 0)
    loads[6].wait()
    k_high[...], k_low[...] = halves(k_raw[...])
    local_part = per_element(first_pre, k_high, k_low) * visc_rows
    first_img = (local_part - coupling * receive(0)) * live_rows
    second_pre = per_element(first_img, p_high, p_low) * inverse_rows
    gather_and_send(second_pre)

    lane = lax.broadcasted_iota(jnp.int32, (1, LANES), 1)

    def note(partial, q, a, b):
        product = a * b
        for p in range(probes):
            column = jnp.sum(product[p * elements : (p + 1) * elements], axis=0, keepdims=True)
            value = jnp.sum(column, axis=1, keepdims=True)
            partial = jnp.where(lane == q * probes + p, value, partial)
        return partial

    partial = jnp.zeros((1, LANES), f32)
    partial = note(partial, 0, first_img, first_img)
    partial = note(partial, 3, first_img, source)
    local_part = per_element(second_pre, k_high, k_low) * visc_rows
    second_img = (local_part - coupling * receive(1)) * live_rows
    partial = note(partial, 1, first_img, second_img)
    partial = note(partial, 2, second_img, second_img)
    partial = note(partial, 4, second_img, source)

    def all_sum(buffer, mine, count, stage, device_of, part, left):
        buffer[mine] = part

        def send(j, carry):
            pltpu.make_async_remote_copy(
                src_ref=buffer.at[mine],
                dst_ref=buffer.at[mine],
                send_sem=send_sems.at[2 + stage],
                recv_sem=sum_sems.at[stage],
                device_id=device_of(j),
                device_id_type=MESH,
            ).start()
            return carry

        lax.fori_loop(0, count - 1, send, 0)
        for gone, sem in left:
            land(gone, send_sems.at[sem], nz - 1)
        land(buffer, sum_sems.at[stage], count - 1)
        total = buffer[0]
        for s in range(1, count):
            total = total + buffer[s]
        return total

    def xy_device(j):
        other = xy_peer(j)
        return (other // ny, other % ny, me)

    total = all_sum(sums_z, me, nz, 0, lambda j: (ix, iy, z_peer(j)), partial, ((departing.at[0], 0), (departing.at[1], 1)))
    total = all_sum(sums_xy, plane, nxy, 1, xy_device, total, ((sums_z, 2),))

    for p in range(probes):
        self_one, cross_mid, self_two, load_one, load_two = (
            jnp.sum(jnp.where(lane == q * probes + p, total, 0.0), axis=1, keepdims=True) for q in range(5)
        )
        determinant = self_one * self_two - cross_mid * cross_mid
        weight_one = (self_two * load_one - cross_mid * load_two) / determinant
        weight_two = (self_one * load_two - cross_mid * load_one) / determinant
        part = slice(p * elements, (p + 1) * elements)
        out_ref[part] = weight_one * first_pre[part] + weight_two * second_pre[part]

    land(sums_xy, send_sems.at[3], nxy - 1)


def solution(mesh):
    nx, ny, nz = (mesh.shape[name] for name in ("gx", "gy", "gz"))

    def per_device(rhs, viscosity, counts, neighbours, face_index, k_matrix, p_matrix):
        probes, elements, dofs = rhs.shape[3:]
        slots, width = face_index.shape[3:]
        rows = probes * elements
        vmem = pltpu.VMEM
        stay = functools.partial(pltpu.with_memory_space_constraint, memory_space=pltpu.HBM)
        hbm = pl.BlockSpec(memory_space=pltpu.HBM)
        half = nz // 4
        out = pl.pallas_call(
            functools.partial(kernel, nx, ny, nz, slots, probes, elements, dofs, width),
            out_shape=jax.ShapeDtypeStruct((rows, dofs), f32),
            in_specs=[hbm] * 7,
            out_specs=pl.BlockSpec(memory_space=vmem),
            scratch_shapes=[
                vmem((rows, dofs), f32),
                vmem((1, elements), f32),
                vmem((1, 1), jnp.int32),
                vmem((1, slots), jnp.int32),
                vmem((slots, width), jnp.int32),
                vmem((dofs, dofs), f32),
                vmem((dofs, dofs), f32),
                vmem((dofs, dofs), bf16),
                vmem((dofs, dofs), bf16),
                vmem((dofs, dofs), bf16),
                vmem((dofs, dofs), bf16),
                vmem((nz, width), jnp.int32),
                vmem((half, dofs, 4 * width), bf16),
                vmem((half, 4 * width, dofs), bf16),
                vmem((slots, 8, LANES), f32),
                vmem((2, nz, 8, LANES), f32),
                vmem((2, nz, 8, LANES), f32),
                vmem((2 * rows, dofs), f32),
                vmem((nz, 1, LANES), f32),
                vmem((nx * ny, 1, LANES), f32),
                pltpu.SemaphoreType.DMA((7,)),
                pltpu.SemaphoreType.DMA((4,)),
                pltpu.SemaphoreType.DMA((2, half + 1)),
                pltpu.SemaphoreType.DMA((2,)),
            ],
            compiler_params=pltpu.CompilerParams(collective_id=0, has_side_effects=True, vmem_limit_bytes=24 * 1024 * 1024),
        )(
            stay(rhs.reshape(rows, dofs)),
            stay(viscosity.reshape(1, elements)),
            counts.reshape(1, 1),
            stay(neighbours.reshape(1, slots)),
            stay(face_index.reshape(slots, width)),
            stay(k_matrix),
            stay(p_matrix),
        )
        return out.reshape(rhs.shape)

    return jax.shard_map(
        per_device,
        mesh=mesh,
        in_specs=(
            P("gx", "gy", "gz", None, None, None),
            P("gx", "gy", "gz", None),
            P("gx", "gy", "gz"),
            P("gx", "gy", "gz", None),
            P("gx", "gy", "gz", None, None),
            P(),
            P(),
        ),
        out_specs=P("gx", "gy", "gz", None, None, None),
        check_vma=False,
    )
```
